32 devices in a mesh: row: 8 (over z, core), col: 4 (over y, x).
Axes of the slice: x: 2, y: 2, z: 4, core: 2. Of those that a mesh axis runs over, the one named last changes fastest.
Arguments:
- features: bfloat16 [64, 512, 512], P(None, 'row', 'col'), may hold values from -60 to 60
- memberships: bfloat16 [16, 512, 512], P(None, 'row', 'col'), may hold values from 0 to 1, as said below
- validity: int32 [512, 512], P('row', 'col'), may hold values 0 or 1
Outputs:
- new_memberships: bfloat16 [16, 512, 512], P(None, 'row', 'col')
- centers: float32 [16, 64], replicated
The draws below stay inside these ranges and needn't reach their ends.
Inputs may be any that keep to these rules, and one draw needn't show every extreme that they name: memberships are positive and a pixel's memberships over the 16 zones sum to 1 up to rounding.
All inputs are finite; a program needn't handle non-finite values. No bound on the sum of `validity` on one device may be relied on, other than what follows from the above.
Results may differ from the reference program's by a relative error of at most 0.004.
Values may be sent and summed in bfloat16 or wider, within the bound.
No kernel may reach another device: no remote copies, remote signals or barrier semaphores. Data moves between devices by JAX's collectives and lax.ppermute only.
A program may use at most 64 MiB of HBM per device.

```python
import math
from functools import partial
import jax
import jax.numpy as jnp
from jax import lax

ZONES = 16
BANDS = 64
HEIGHT = 512
WIDTH = 512


def membership_field(key):
    key_list = jax.random.split(jax.random.fold_in(key, 23), 4)
    rows_pos = jnp.arange(HEIGHT, dtype=jnp.float32)[None, :, None] / HEIGHT
    cols_pos = jnp.arange(WIDTH, dtype=jnp.float32)[None, None, :] / WIDTH
    freq_rows = jax.random.randint(key_list[0], (ZONES, 1, 1), 1, 4).astype(jnp.float32)
    freq_cols = jax.random.randint(key_list[1], (ZONES, 1, 1), 1, 4).astype(jnp.float32)
    phases = jax.random.uniform(key_list[2], (ZONES, 1, 1), minval=-math.pi, maxval=math.pi)
    noise_field = 3.5 * jax.random.normal(key_list[3], (ZONES, HEIGHT, WIDTH))
    logits = noise_field + 1.5 * jnp.sin(2.0 * math.pi * (freq_rows * rows_pos + freq_cols * cols_pos) + phases)
    shifted = logits - jnp.max(logits, axis=0, keepdims=True)
    expo_field = jnp.exp(shifted)
    return expo_field / jnp.sum(expo_field, axis=0, keepdims=True)


def draw_memberships(key, part):
    return membership_field(key).astype(jnp.bfloat16)


def draw_features(key, part):
    key_list = jax.random.split(jax.random.fold_in(key, 11), 6)
    zone_rates = jax.random.uniform(jax.random.fold_in(key, 37), (ZONES, BANDS), minval=-math.log(3.0), maxval=math.log(3.0))
    probs = membership_field(key)
    rows_pos = jnp.arange(HEIGHT, dtype=jnp.float32)[None, :, None] / HEIGHT
    cols_pos = jnp.arange(WIDTH, dtype=jnp.float32)[None, None, :] / WIDTH
    freq_rows = jax.random.randint(key_list[0], (BANDS, 1, 1), 1, 5).astype(jnp.float32)
    freq_cols = jax.random.randint(key_list[1], (BANDS, 1, 1), 1, 5).astype(jnp.float32)
    phases = jax.random.uniform(key_list[2], (BANDS, 1, 1), minval=-math.pi, maxval=math.pi)
    amplitude = jax.random.uniform(key_list[3], (BANDS, 1, 1), minval=1.0, maxval=2.5)
    band_scale = jnp.exp(jax.random.uniform(key_list[4], (BANDS, 1, 1), minval=math.log(0.25), maxval=math.log(1.33)))
    noise_field = jnp.clip(jax.random.normal(key_list[5], (BANDS, HEIGHT, WIDTH)), -6.0, 6.0)
    mixed_noise = noise_field + 0.6 * jnp.roll(noise_field, 1, axis=0) + 0.3 * jnp.roll(noise_field, 2, axis=0)
    log_factor = jnp.zeros((BANDS, HEIGHT, WIDTH), dtype=jnp.float32)
    for zone_index in range(ZONES):
        log_factor = log_factor + zone_rates[zone_index][:, None, None] * probs[zone_index][None]
    zone_noise = mixed_noise * jnp.exp(log_factor)
    smooth_part = amplitude * jnp.sin(2.0 * math.pi * (freq_rows * rows_pos + freq_cols * cols_pos) + phases)
    return (band_scale * (zone_noise + smooth_part)).astype(jnp.bfloat16)


def plant(array, own_key, low, top_value):
    spot = [jax.random.randint(jax.random.fold_in(own_key, axis), (), 0, length) for axis, length in enumerate(array.shape)]
    longest = array.shape.index(max(array.shape))
    neighbour = spot[:longest] + [(spot[longest] + 1) % array.shape[longest]] + spot[longest + 1:]
    return array.at[tuple(spot)].set(low).at[tuple(neighbour)].set(top_value)


def setup_inputs(seed: int = 0) -> dict:
    arg_keys = jax.random.split(jax.random.key(seed), 4)
    return {
        "features": draw_features(jax.random.fold_in(arg_keys[3], 71), 0),
        "memberships": draw_memberships(jax.random.fold_in(arg_keys[3], 71), 0),
        "validity": plant((jax.random.randint(arg_keys[2], (HEIGHT, WIDTH), 0, 8) < 7).astype(jnp.int32), jax.random.fold_in(arg_keys[2], 1), 0, 1),
    }


ridge_term = 0.01
penalty_weight = 3.0
cost_offset = 0.05

def zone_moments(flat_features, weight_row):
    scaled = (weight_row.astype(jnp.float32)[None, :] * flat_features.astype(jnp.float32)).astype(jnp.bfloat16)
    second_moment = lax.dot_general(scaled.astype(jnp.float32), scaled.astype(jnp.float32), (((1,), (1,)), ((), ())), preferred_element_type=jnp.float32)
    first_moment = jnp.dot(scaled.astype(jnp.float32), weight_row.astype(jnp.float32), preferred_element_type=jnp.float32)
    weight_sum = jnp.sum(jnp.square(weight_row.astype(jnp.float32)))
    return (weight_sum, first_moment, second_moment)

def whitening(covariance):
    dimension = covariance.shape[0]
    factor = jnp.linalg.cholesky(covariance)
    scale_det = jnp.exp(2.0 * jnp.sum(jnp.log(jnp.diagonal(factor))) / dimension)
    identity = jnp.eye(dimension, dtype=jnp.float32)
    inverse = lax.linalg.triangular_solve(factor, identity, left_side=True, lower=True)
    return (jnp.sqrt(scale_det) * inverse).astype(jnp.bfloat16)

def factor_zones(zone_counts, first_moment, second_moment):
    dimension = first_moment.shape[1]
    centers = first_moment / zone_counts[:, None]
    covariance = second_moment / zone_counts[:, None, None] - centers[:, :, None] * centers[:, None, :]
    covariance = covariance + ridge_term * jnp.eye(dimension, dtype=jnp.float32)
    white_mats = lax.map(whitening, covariance)
    white_centers = jnp.einsum('kfg,kg->kf', white_mats.astype(jnp.float32), centers, precision=lax.Precision.HIGHEST)
    return (white_mats, white_centers, centers)

def zone_distance(flat_features, zone_pair):
    white_mat, white_center = zone_pair
    projected = jnp.dot(white_mat.astype(jnp.float32), flat_features.astype(jnp.float32), preferred_element_type=jnp.float32)
    return lax.optimization_barrier(jnp.sum(jnp.square(projected - white_center[:, None]), axis=0))

def reference(features, memberships, validity):
    num_bands, height_px, width_px = features.shape
    num_zones = memberships.shape[0]
    valid_map = validity.astype(jnp.float32)
    member_f = memberships.astype(jnp.float32)
    weights_bf = (member_f * valid_map[None]).astype(jnp.bfloat16)
    flat_features = features.reshape(num_bands, height_px * width_px)
    flat_weights = weights_bf.reshape(num_zones, height_px * width_px)
    zone_counts, first_moment, second_moment = lax.map(partial(zone_moments, flat_features), flat_weights)
    white_mats, white_centers, centers = factor_zones(zone_counts, first_moment, second_moment)
    distance = lax.map(partial(zone_distance, flat_features), (white_mats, white_centers))
    distance = distance.reshape(num_zones, height_px, width_px)
    penalty_terms = (valid_map[None] * jnp.square(1.0 - member_f)).astype(jnp.bfloat16)
    stacked = jnp.concatenate([penalty_terms, valid_map[None].astype(jnp.bfloat16)], axis=0).astype(jnp.float32)
    padded = jnp.pad(stacked, ((0, 0), (1, 1), (1, 1)))
    neighbours = padded[:, :-2, 1:-1] + padded[:, 2:, 1:-1] + padded[:, 1:-1, :-2] + padded[:, 1:-1, 2:]
    penalty = neighbours[:num_zones] / jnp.maximum(neighbours[num_zones], 1.0)[None]
    cost_total = distance / num_bands + penalty_weight * penalty + cost_offset
    inverse = 1.0 / cost_total
    new_memberships = (valid_map[None] * inverse / lax.optimization_barrier(jnp.sum(inverse, axis=0, keepdims=True))).astype(jnp.bfloat16)
    return (new_memberships, centers)
```

```python
import functools

import jax
import jax.numpy as jnp
from jax import lax
from jax.experimental import pallas as pl
from jax.experimental.pallas import tpu as pltpu
from jax.sharding import PartitionSpec as P

ridge_term = 0.01
penalty_weight = 3.0
cost_offset = 0.05

F32 = jnp.float32
BF16 = jnp.bfloat16
LANES = 128
GROUP = 8


def full_spec():
    return pl.BlockSpec(memory_space=pltpu.VMEM)


def params(mebibytes):
    return pltpu.CompilerParams(vmem_limit_bytes=mebibytes << 20)


def core_half():
    return lax.rem(lax.axis_index("row"), 2)


def moments_kernel(
    feat_ref, memb_ref, valid_ref,
    keep_ref, send_ref, top_ref, bottom_ref, left_ref, right_ref,
    square_ref, lhs_ref, acc_ref,
):
    zones, rows, cols = memb_ref.shape
    bands = feat_ref.shape[1]
    half = zones // 2
    valid = valid_ref[...].astype(F32)
    lane_col = lax.broadcasted_iota(jnp.int32, (rows, LANES), 1)
    left = jnp.where(lane_col == zones, valid[:, 0:1], 0.0)
    right = jnp.where(lane_col == zones, valid[:, cols - 1 : cols], 0.0)
    top_ref[zones : zones + 1, :] = valid[0:1].astype(BF16)
    bottom_ref[zones : zones + 1, :] = valid[rows - 1 : rows].astype(BF16)
    for k in range(zones):
        member = memb_ref[k].astype(F32)
        weight = member * valid
        square_ref[k] = weight * weight
        term = valid * jnp.square(1.0 - member)
        left = jnp.where(lane_col == k, term[:, 0:1], left)
        right = jnp.where(lane_col == k, term[:, cols - 1 : cols], right)
        top_ref[k : k + 1, :] = term[0:1].astype(BF16)
        bottom_ref[k : k + 1, :] = term[rows - 1 : rows].astype(BF16)
    left_ref[...] = left.astype(BF16)
    right_ref[...] = right.astype(BF16)
    acc_ref[...] = jnp.zeros_like(acc_ref)

    def group_step(g, carry):
        base = pl.multiple_of(g * GROUP, GROUP)
        rhs = []
        for r in range(GROUP):
            tile = feat_ref[base + r]
            rhs.append(tile)
            for k in range(zones):
                row = square_ref[k, pl.ds(base + r, 1), :]
                wide = jnp.broadcast_to(row, (bands, cols)).astype(BF16)
                lhs_ref[k * bands : (k + 1) * bands, r * cols : (r + 1) * cols] = wide * tile
            lhs_ref[zones * bands :, r * cols : (r + 1) * cols] = square_ref[
                :, base + r, :
            ].astype(BF16)
        rhs = jnp.concatenate(rhs, axis=1)
        rhs = jnp.concatenate([rhs, jnp.ones((LANES - bands, GROUP * cols), BF16)], axis=0)
        acc_ref[...] += lax.dot_general(
            lhs_ref[...], rhs, (((1,), (1,)), ((), ())), preferred_element_type=F32
        )
        return carry

    lax.fori_loop(0, rows // GROUP, group_step, 0)

    row_i = lax.broadcasted_iota(jnp.int32, (bands, LANES), 0)
    lane_i = lax.broadcasted_iota(jnp.int32, (bands, LANES), 1)
    means = acc_ref[zones * bands :, :]
    zone_row = lax.broadcasted_iota(jnp.int32, (zones, LANES), 0)
    zone_lane = lax.broadcasted_iota(jnp.int32, (zones, LANES), 1)
    diags = jnp.zeros((zones, LANES), F32)
    for k in range(1, zones, 2):
        block = acc_ref[k * bands : (k + 1) * bands, :]
        diag = jnp.sum(jnp.where(lane_i == row_i, block, 0.0), axis=0, keepdims=True)
        diags = jnp.where(zone_row == k, diag, diags)
    diags = pltpu.roll(diags, bands, 1)
    after = pltpu.roll(means, zones - 1, 0)
    even = jnp.where(zone_lane >= bands + bands // 2, after, means)
    odd = jnp.where(zone_lane >= bands, diags, means)
    extra = jnp.where(lax.rem(zone_row, 2) == 0, even, odd)

    me = core_half()
    for out_ref, h in ((keep_ref, me), (send_ref, 1 - me)):
        for b in range(half // 4):

            def zone_block(q):
                start = pl.multiple_of((h * half + 4 * b + q) * bands, bands)
                return acc_ref[pl.ds(start, bands), :]

            first = jnp.where(lane_i <= row_i, zone_block(0), zone_block(1))
            second = jnp.where(lane_i <= row_i, zone_block(2), zone_block(3))
            out_ref[b * bands : (b + 1) * bands, :] = jnp.where(
                lane_i < bands, first, pltpu.roll(second, bands, 1)
            )
        out_ref[half // 4 * bands :, :] = extra


def factor_kernel(sums_ref, white_ref, centers_ref, mat_ref):
    zones, bands = centers_ref.shape
    half = zones // 2
    base = half // 4 * bands
    extra = sums_ref[base : base + zones, :]
    lane_e = lax.broadcasted_iota(jnp.int32, (zones, LANES), 1)
    row_e = lax.broadcasted_iota(jnp.int32, (zones, LANES), 0)
    even_count = extra[:, bands : bands + 1]
    odd_count = pltpu.roll(
        jnp.broadcast_to(extra[:, bands + bands // 2 : bands + bands // 2 + 1], (zones, LANES)), 1, 0
    )
    counts = jnp.where(lax.rem(row_e, 2) == 0, even_count, odd_count)
    centers_ref[...] = (extra / counts)[:, :bands]

    me = core_half()
    mine = sums_ref[pl.ds(pl.multiple_of(base + me * half, half), half), :]
    row_i = lax.broadcasted_iota(jnp.int32, (bands, LANES), 0)
    lane_i = lax.broadcasted_iota(jnp.int32, (bands, LANES), 1)
    eye = jnp.where(lane_i == row_i, 1.0, 0.0).astype(F32)
    right_eye = jnp.where(lane_i == row_i + bands, 1.0, 0.0).astype(F32)
    mine_t = jnp.transpose(jnp.concatenate([mine, jnp.zeros((LANES - half, LANES), F32)], axis=0))
    packed = sums_ref[0:base, :]
    packed_t = jnp.transpose(packed)
    center_rows = []
    for z in range(half):
        pair, odd = z // 2, z % 2
        b, side = pair // 2, pair % 2
        upper = packed[b * bands : (b + 1) * bands, :]
        lower = packed_t[side * bands : (side + 1) * bands, :]
        if side:
            upper = pltpu.roll(upper, bands, 1)
        if b:
            lower = pltpu.roll(lower, bands, 1)
        count_lane = bands if odd == 0 else bands + bands // 2
        count = mine[z - odd : z - odd + 1, count_lane : count_lane + 1]
        center = mine[z : z + 1, :] / count
        column = mine_t[0:bands, z : z + 1] / count
        if odd == 0:
            second = jnp.where(lane_i <= row_i, upper, lower)
        else:
            diag = pltpu.roll(mine[z : z + 1, :], bands, 1)
            second = jnp.where(lane_i > row_i, upper, lower)
            second = jnp.where(lane_i == row_i, diag, second)
        covariance = second / count - column * center + ridge_term * eye
        mat_ref[z] = jnp.where(lane_i < bands, covariance, right_eye)
        center_rows.append(center)

    sub = lax.broadcasted_iota(jnp.int32, (8, LANES), 0)
    blocks = bands // 8
    for kb in range(blocks):

        def step(j, carry):
            k = kb * 8 + 2 * j
            at_first = jnp.full((8, LANES), k, jnp.int32)
            at_second = at_first + 1
            below_first = sub > 2 * j
            below_second = sub > 2 * j + 1
            pivots = []
            for z in range(half):
                first = jnp.broadcast_to(mat_ref[z, pl.ds(k, 1), :], (8, LANES))
                second = jnp.broadcast_to(mat_ref[z, pl.ds(k + 1, 1), :], (8, LANES))
                pivot = jnp.take_along_axis(first, at_first, axis=1)
                cross = jnp.take_along_axis(first, at_second, axis=1)
                under = jnp.take_along_axis(second, at_first, axis=1)
                corner = jnp.take_along_axis(second, at_second, axis=1)
                ratio = cross / pivot
                first = first / pivot
                second = second - under * first
                second = second / (corner - under * ratio)
                pivots.append((first, second, ratio))
            for z in range(half):
                first, second, ratio = pivots[z]
                for rb in range(kb, blocks):
                    block = mat_ref[z, rb * 8 : (rb + 1) * 8, :]
                    left = jnp.take_along_axis(block, at_first, axis=1)
                    right = jnp.take_along_axis(block, at_second, axis=1) - left * ratio
                    if rb == kb:
                        left = jnp.where(below_first, left, 0.0)
                        right = jnp.where(below_second, right, 0.0)
                    mat_ref[z, rb * 8 : (rb + 1) * 8, :] = block - left * first - right * second
            return carry

        lax.fori_loop(0, 4, step, 0)

    for z in range(half):
        mat = mat_ref[z]
        pivots = jnp.sum(mat * eye, axis=1, keepdims=True)
        log_det = jnp.sum(jnp.log(pivots), axis=0, keepdims=True)
        scale = jnp.exp(0.5 * log_det / bands) * lax.rsqrt(pivots)
        white = pltpu.roll(mat, bands, 1) * scale
        white = jnp.where(lane_i < bands, white, 0.0).astype(BF16)
        shift = -jnp.sum(white.astype(F32) * center_rows[z], axis=1, keepdims=True)
        hi = shift.astype(BF16)
        mid = (shift - hi.astype(F32)).astype(BF16)
        low = (shift - hi.astype(F32) - mid.astype(F32)).astype(BF16)
        tail = jnp.where(lane_i == bands, hi.astype(F32), 0.0)
        tail = jnp.where(lane_i == bands + 1, mid.astype(F32), tail)
        tail = jnp.where(lane_i == bands + 2, low.astype(F32), tail)
        white_ref[z * bands : (z + 1) * bands, :] = (white.astype(F32) + tail).astype(BF16)


def penalty_kernel(memb_ref, valid_ref, above_ref, below_ref, left_ref, right_ref, out_ref):
    zones, rows, cols = memb_ref.shape
    valid = valid_ref[...].astype(F32)
    row_i = lax.broadcasted_iota(jnp.int32, (rows, cols), 0)
    lane_i = lax.broadcasted_iota(jnp.int32, (rows, cols), 1)
    above = above_ref[...].astype(F32)
    below = below_ref[...].astype(F32)
    left = left_ref[...].astype(F32)
    right = right_ref[...].astype(F32)

    def neighbours(x, k):
        up = jnp.where(row_i == 0, above[k : k + 1, :], pltpu.roll(x, 1, 0))
        down = jnp.where(row_i == rows - 1, below[k : k + 1, :], pltpu.roll(x, rows - 1, 0))
        west = jnp.where(lane_i == 0, left[:, k : k + 1], pltpu.roll(x, 1, 1))
        east = jnp.where(lane_i == cols - 1, right[:, k : k + 1], pltpu.roll(x, cols - 1, 1))
        return up + down + west + east

    scale = penalty_weight / jnp.maximum(neighbours(valid, zones), 1.0)
    for k in range(zones):
        member = memb_ref[k].astype(F32)
        term = (valid * jnp.square(1.0 - member)).astype(BF16).astype(F32)
        out_ref[k] = neighbours(term, k) * scale + cost_offset


def update_kernel(
    feat_ref, valid_ref, mine_ref, other_ref, penalty_ref, out_ref, white_ref, part_ref
):
    zones, rows, cols = penalty_ref.shape
    bands = feat_ref.shape[1]
    half = zones // 2
    me = core_half()
    span = half * bands
    white_ref[pl.ds(pl.multiple_of(me * span, span), span), :] = mine_ref[...]
    white_ref[pl.ds(pl.multiple_of((1 - me) * span, span), span), :] = other_ref[...]
    ones = jnp.ones((LANES - bands, 2 * cols), BF16)

    def group_step(g, carry):
        base = pl.multiple_of(g * GROUP, GROUP)
        for t in range(GROUP // 2):
            pixels = jnp.concatenate([feat_ref[base + 2 * t], feat_ref[base + 2 * t + 1]], axis=1)
            pixels = jnp.concatenate([pixels, ones], axis=0)
            projected = jnp.dot(white_ref[...], pixels, preferred_element_type=F32)
            squares = jnp.square(projected).reshape(zones, bands // 8, 8, 2 * cols)
            partial = jnp.sum(squares, axis=1)
            part_ref[:, 2 * t] = partial[:, :, :cols]
            part_ref[:, 2 * t + 1] = partial[:, :, cols:]
        total = jnp.zeros((GROUP, cols), F32)
        inverses = []
        for k in range(zones):
            distance = jnp.sum(part_ref[k], axis=1)
            cost = distance * (1.0 / bands) + penalty_ref[k, pl.ds(base, GROUP), :]
            inverse = 1.0 / cost
            inverses.append(inverse)
            total = total + inverse
        ratio = valid_ref[pl.ds(base, GROUP), :].astype(F32) / total
        for k in range(zones):
            out_ref[k, pl.ds(base, GROUP), :] = (inverses[k] * ratio).astype(BF16)
        return carry

    lax.fori_loop(0, rows // GROUP, group_step, 0)


def swap(value, axis, bit):
    count = lax.axis_size(axis)
    return lax.ppermute(value, axis, [(i, i ^ bit) for i in range(count)])


def shift(value, axis, step):
    count = lax.axis_size(axis)
    return lax.ppermute(
        value, axis, [(i, i + step) for i in range(count) if 0 <= i + step < count]
    )


def on_device(features, memberships, validity):
    bands, rows, cols = features.shape
    zones = memberships.shape[0]
    half = zones // 2
    shape = jax.ShapeDtypeStruct
    pixels = features.transpose(1, 0, 2)
    sums_shape = shape((half // 4 * bands + zones, LANES), F32)
    row_edge = shape((zones + 1, cols), BF16)
    col_edge = shape((rows, LANES), BF16)
    keep, send, top, bottom, left, right = pl.pallas_call(
        moments_kernel,
        out_shape=(sums_shape, sums_shape, row_edge, row_edge, col_edge, col_edge),
        in_specs=[full_spec()] * 3,
        out_specs=(full_spec(),) * 6,
        scratch_shapes=[
            pltpu.VMEM((zones, rows, cols), F32),
            pltpu.VMEM((zones * (bands + 1), GROUP * cols), BF16),
            pltpu.VMEM((zones * (bands + 1), LANES), F32),
        ],
        compiler_params=params(24),
        name="moments",
    )(pixels, memberships, validity)
    sums = keep + swap(send, "row", 1)
    for axis in ("col", "row"):
        bit = 1 if axis == "col" else 2
        while bit < lax.axis_size(axis):
            sums = sums + swap(sums, axis, bit)
            bit *= 2
    above = shift(bottom, "row", 1)
    below = shift(top, "row", -1)
    west = shift(right, "col", 1)
    east = shift(left, "col", -1)
    penalty = pl.pallas_call(
        penalty_kernel,
        out_shape=shape((zones, rows, cols), F32),
        in_specs=[full_spec()] * 6,
        out_specs=full_spec(),
        compiler_params=params(8),
        name="penalty",
    )(memberships, validity, above, below, west, east)
    white, centers = pl.pallas_call(
        factor_kernel,
        out_shape=(shape((half * bands, LANES), BF16), shape((zones, bands), F32)),
        in_specs=[full_spec()],
        out_specs=(full_spec(),) * 2,
        scratch_shapes=[pltpu.VMEM((half, bands, LANES), F32)],
        compiler_params=params(8),
        name="factor",
    )(sums)
    other = swap(white, "row", 1)
    new_memberships = pl.pallas_call(
        update_kernel,
        out_shape=shape((zones, rows, cols), BF16),
        in_specs=[full_spec()] * 5,
        out_specs=full_spec(),
        scratch_shapes=[
            pltpu.VMEM((zones * bands, LANES), BF16),
            pltpu.VMEM((zones, GROUP, 8, cols), F32),
        ],
        compiler_params=params(24),
        name="update",
    )(pixels, validity, white, other, penalty)
    return (new_memberships, centers)


def solution(mesh):
    return jax.shard_map(
        on_device,
        mesh=mesh,
        in_specs=(P(None, "row", "col"), P(None, "row", "col"), P("row", "col")),
        out_specs=(P(None, "row", "col"), P()),
        check_vma=False,
    )
```
